32 devices in a mesh: row: 8 (over z, y), col: 4 (over x, core).
Axes of the slice: x: 2, y: 2, z: 4, core: 2. Of those that a mesh axis runs over, the one named last changes fastest.
Arguments:
- kernel_configs: float32 [4, 512, 2048], P(None, 'row', 'col'), may hold values from -1 to 2, as said below
- epoch_kernel: float32 [256, 256], replicated, may hold values from -1 to 2, as said below
- lengths: int32 [2048], P(('col', 'row')), may hold values from 1 to 256
- noise: float32 [2048], P(('col', 'row')), may hold values from 0.1 to 1
- curves: float32 [2048, 256], P(('col', 'row')), may hold values from -33 to 33
Outputs:
- solution: float32 [2048, 256], P(('col', 'row'))
- residual: float32 [2048, 256], P(('col', 'row'))
The draws below stay inside these ranges and needn't reach their ends.
Inputs may be any that keep to these rules, and one draw needn't show every extreme that they name: `kernel_configs`: reshaped to 2048 x 2048 by merging the first two dimensions, the matrix is symmetric positive definite. `epoch_kernel`: symmetric positive definite.
All inputs are finite; a program needn't handle non-finite values.
Results may differ from the reference program's by a relative error of at most 0.00026.
Values sent between devices are 32-bit elements; how exact they have to be, the bound alone decides.
A program may use at most 64 MiB of HBM per device.

```python
import math
import jax
import jax.numpy as jnp
from jax import lax

E = 256
ITERS = 2
N = 2048
COLBLK = 512
NCB = 4


def symmetric_draw(key, order):
    values = jax.random.normal(key, (order, order), jnp.float32)
    spread = 0.4 / math.sqrt(2.0 * order)
    return jnp.eye(order, dtype=jnp.float32) + spread * (values + values.T)


def draw_kernel_configs(key, part):
    full_matrix = symmetric_draw(jax.random.fold_in(key, 11), N)
    return full_matrix.reshape(NCB, COLBLK, N)


def draw_epoch_kernel(key, part):
    return symmetric_draw(jax.random.fold_in(key, 13), E)


def draw_lengths(key, part):
    first_key, second_key = jax.random.split(jax.random.fold_in(key, 17))
    tier = jax.random.randint(first_key, (N,), 0, 16)
    shift = (tier >= 8).astype(jnp.int32) + (tier >= 12).astype(jnp.int32) + (tier >= 14).astype(jnp.int32) + (tier >= 15).astype(jnp.int32)
    top_length = jnp.right_shift(jnp.full((N,), E, jnp.int32), shift)
    dropped = jax.random.randint(second_key, (N,), 0, jnp.maximum(top_length // 2, 1))
    return (top_length - dropped).at[0].set(E).astype(jnp.int32)


def draw_curves(key, part):
    first_key, second_key = jax.random.split(jax.random.fold_in(key, 19))
    base_values = jax.random.truncated_normal(first_key, -6.0, 6.0, (N, E), jnp.float32)
    level = jax.random.uniform(second_key, (N, 1), jnp.float32)
    position = jnp.arange(N, dtype=jnp.float32)[:, None] / N
    row_scale = jnp.power(10.0, level - 0.5) * jnp.power(3.0, position - 0.5)
    return base_values * row_scale


def block_scale(own_key, dims, cuts, smallest, top_value):
    def one(dim, blocks):
        steps = jax.random.uniform(jax.random.fold_in(jax.random.fold_in(own_key, 6), dim), (blocks,), jnp.float32, smallest / len(cuts), top_value / len(cuts))
        return jnp.repeat(jnp.exp(steps), dims[dim] // blocks).reshape((-1,) + (1,) * (len(dims) - dim - 1))

    gain = one(*cuts[0])
    for cut in cuts[1:]:
        gain = gain * one(*cut)
    return gain


def setup_inputs(seed: int = 0) -> dict:
    splits = jax.random.split(jax.random.key(seed), 6)
    return {
        "kernel_configs": draw_kernel_configs(jax.random.fold_in(splits[5], 71), 0),
        "epoch_kernel": draw_epoch_kernel(jax.random.fold_in(splits[5], 71), 0),
        "lengths": draw_lengths(jax.random.fold_in(splits[5], 71), 0),
        "noise": jnp.clip(jnp.exp(math.log(1.0) - 2.3025851 * jax.random.uniform(splits[3], (N,), jnp.float32) ** block_scale(splits[3], (N,), ((0, 32),), -0.2, 0.2)), 0.1, 1.0),
        "curves": draw_curves(jax.random.fold_in(splits[5], 71), 0),
    }


def apply_operator(vector, kernel_full, epoch_kernel, curve_mask, noise):
    masked = vector * curve_mask
    summed = jnp.dot(kernel_full, masked, precision=lax.Precision.HIGHEST, preferred_element_type=jnp.float32)
    smoothed = jnp.dot(summed, epoch_kernel, precision=lax.Precision.HIGHEST, preferred_element_type=jnp.float32)
    return curve_mask * smoothed + noise[:, None] * vector


def reference(kernel_configs, epoch_kernel, lengths, noise, curves):
    kernel_full = kernel_configs.reshape(N, N)
    epoch_index = jnp.arange(E, dtype=jnp.int32)
    curve_mask = (epoch_index[None, :] < lengths[:, None]).astype(jnp.float32)
    solution = jnp.zeros_like(curves)
    residual = curves * curve_mask
    direction = residual
    norm_now = jnp.sum(residual * residual)
    for iteration in range(ITERS):
        applied = apply_operator(direction, kernel_full, epoch_kernel, curve_mask, noise)
        step_size = norm_now / jnp.sum(direction * applied)
        solution = solution + step_size * direction
        residual = residual - step_size * applied
        norm_next = jnp.sum(residual * residual)
        direction = residual + (norm_next / norm_now) * direction
        norm_now = norm_next
    return solution, residual
```

```python
import functools

import jax
import jax.numpy as jnp
from jax import lax
from jax.experimental import pallas as pl
from jax.experimental.pallas import tpu as pltpu
from jax.sharding import PartitionSpec as P

MESH = pl.DeviceIdType.MESH
HALVES = 2
INNER = 2


def flip(index, bits):
    place = 1
    result = index
    while place <= bits:
        if (bits // place) % 2:
            result = result + place * (1 - 2 * ((index // place) % 2))
        place *= 2
    return result


def split(value):
    high = value.astype(jnp.bfloat16)
    low = (value - high.astype(jnp.float32)).astype(jnp.bfloat16)
    return high, low


def dot3(left, right):
    mul = functools.partial(jnp.dot, preferred_element_type=jnp.float32)
    return mul(left[0], right[0]) + (mul(left[0], right[1]) + mul(left[1], right[0]))


def fold(value):
    rows, epochs = value.shape
    tiles = [
        value[i : i + 8, j : j + 128] for i in range(0, rows, 8) for j in range(0, epochs, 128)
    ]
    while len(tiles) > 1:
        tiles = [sum(tiles[i : i + 2][1:], tiles[i]) for i in range(0, len(tiles), 2)]
    return tiles[0]


def total(tile):
    return jnp.sum(jnp.sum(tile, axis=0, keepdims=True), axis=1, keepdims=True)


def column(row):
    n = row.shape[1]
    one = lax.broadcasted_iota(jnp.int32, (n, n), 0)
    two = lax.broadcasted_iota(jnp.int32, (n, n), 1)
    return jnp.sum(jnp.where(one == two, row, jnp.zeros_like(row)), axis=1, keepdims=True)


def kernel(
    R, C,
    tile_hbm, epoch_hbm, lengths_hbm, noise_hbm, curves_hbm,
    solution_ref, residual_ref,
    tile, epoch, lengths, noise, curves,
    tile_high, tile_low, epoch_high, epoch_low,
    gathered, partial, arrived, sums_col, sums_row,
    load_sem, line_send, line_recv, pair_send, pair_recv,
    part_send, part_recv, col_send, col_recv, row_send, row_recv,
):
    L = R // INNER
    me_row = lax.axis_index("row")
    me_col = lax.axis_index("col")
    outer = me_row // INNER
    inner = me_row % INNER
    other = 1 - inner
    rows, epochs = curves.shape
    width = epochs // HALVES

    loads = []
    for i, (src, dst) in enumerate(
        ((curves_hbm, curves), (lengths_hbm, lengths), (noise_hbm, noise),
         (tile_hbm, tile), (epoch_hbm, epoch))
    ):
        load = pltpu.make_async_copy(src, dst, load_sem.at[i])
        load.start()
        loads.append(load)

    barrier = pltpu.get_barrier_semaphore()
    for k in range(1, R):
        pl.semaphore_signal(barrier, inc=1, device_id=(flip(me_row, k), me_col), device_id_type=MESH)
    for j in range(1, C):
        pl.semaphore_signal(barrier, inc=1, device_id=(me_row, flip(me_col, j)), device_id_type=MESH)

    for load in loads[:3]:
        load.wait()
    length_col = column(lengths[...].astype(jnp.float32))
    noise_col = column(noise[...])
    position = lax.broadcasted_iota(jnp.int32, (rows, epochs), 1).astype(jnp.float32)
    mask = position < length_col
    first = jnp.where(mask, curves[...], 0.0)

    def remote(src, dst, send, recv, target):
        copy = pltpu.make_async_remote_copy(
            src_ref=src, dst_ref=dst, send_sem=send, recv_sem=recv,
            device_id=target, device_id_type=MESH,
        )
        return copy

    def place(op, h, k, side):
        return gathered.at[op, h, flip(outer, k) * INNER + side]

    def line_copy(op, h, k):
        return remote(
            place(op, h, 0, inner), place(op, h, 0, inner),
            line_send.at[op, h, k], line_recv.at[op, h, k],
            (flip(outer, k) * INNER + inner, me_col),
        )

    def line_arrival(op, h, k):
        return remote(
            place(op, h, k, inner), place(op, h, k, inner),
            line_send.at[op, h, k], line_recv.at[op, h, k],
            (flip(outer, k) * INNER + inner, me_col),
        )

    def pair_copy(op, h, k):
        return remote(
            place(op, h, k, inner), place(op, h, k, inner),
            pair_send.at[op, h, k], pair_recv.at[op, h, k],
            (outer * INNER + other, me_col),
        )

    def pair_arrival(op, h, k):
        return remote(
            place(op, h, k, other), place(op, h, k, other),
            pair_send.at[op, h, k], pair_recv.at[op, h, k],
            (outer * INNER + other, me_col),
        )

    def part_copy(op, h, j):
        return remote(
            partial.at[op, h, flip(me_col, j)], arrived.at[op, h, j - 1],
            part_send.at[op, h, j], part_recv.at[op, h, j],
            (me_row, flip(me_col, j)),
        )

    def col_copy(t, j):
        return remote(
            sums_col.at[t, 0], sums_col.at[t, j],
            col_send.at[t, j], col_recv.at[t, j],
            (me_row, flip(me_col, j)),
        )

    def row_copy(t, k):
        return remote(
            sums_row.at[t, 0], sums_row.at[t, k],
            row_send.at[t, k], row_recv.at[t, k],
            (flip(me_row, k), me_col),
        )

    def spread(op, field):
        for h in range(HALVES):
            gathered[op, h, me_row] = field[:, h * width : (h + 1) * width]
            for k in range(1, L):
                line_copy(op, h, k).start()
            pair_copy(op, h, 0).start()

    def relay(op):
        for h in range(HALVES):
            for k in range(1, L):
                line_arrival(op, h, k).wait_recv()
                pair_copy(op, h, k).start()

    def multiply(op):
        for h in range(HALVES):
            for k in range(L):
                pair_arrival(op, h, k).wait_recv()
            block = split(gathered[op, h].reshape(R * rows, width))
            product = dot3((tile_high[...], tile_low[...]), block)
            partial[op, h] = product.reshape(C, rows, width)
            for j in range(1, C):
                part_copy(op, h, j).start()

    def finish(op, field):
        smoothed = None
        for h in range(HALVES):
            value = partial[op, h, me_col]
            for j in range(1, C):
                part_copy(op, h, j).wait_recv()
                value = value + arrived[op, h, j - 1]
            cut = slice(h * width, (h + 1) * width)
            term = dot3(split(value), (epoch_high[cut, :], epoch_low[cut, :]))
            smoothed = term if smoothed is None else smoothed + term
        return jnp.where(mask, smoothed, 0.0) + noise_col * field

    def drain(op):
        for h in range(HALVES):
            for k in range(1, L):
                line_copy(op, h, k).wait_send()
            for k in range(L):
                pair_copy(op, h, k).wait_send()
            for j in range(1, C):
                part_copy(op, h, j).wait_send()

    def sums_start(t, one, two):
        sums_col[t, 0, 0] = fold(one)
        sums_col[t, 0, 1] = fold(two)
        for j in range(1, C):
            col_copy(t, j).start()

    def sums_pass(t):
        for j in range(1, C):
            col_copy(t, j).wait_recv()
        value = sums_col[t, 0]
        for j in range(1, C):
            value = value + sums_col[t, j]
        sums_row[t, 0] = value
        for k in range(1, R):
            row_copy(t, k).start()

    def sums_end(t):
        for k in range(1, R):
            row_copy(t, k).wait_recv()
        value = sums_row[t, 0]
        for k in range(1, R):
            value = value + sums_row[t, k]
        return total(value[0]), total(value[1])

    def sums_drain(t):
        for j in range(1, C):
            col_copy(t, j).wait_send()
        for k in range(1, R):
            row_copy(t, k).wait_send()

    pl.semaphore_wait(barrier, R - 1 + C - 1)
    spread(0, first)
    for load in loads[3:]:
        load.wait()
    high, low = split(tile[...].reshape(C * rows, R * rows))
    tile_high[...] = high
    tile_low[...] = low
    high, low = split(epoch[...])
    epoch_high[...] = high
    epoch_low[...] = low
    relay(0)
    multiply(0)
    image = finish(0, first)

    spread(1, image)
    sums_start(0, first * first, first * image)
    sums_pass(0)
    relay(1)
    norm_first, curvature = sums_end(0)
    step = norm_first / curvature
    second = first - step * image
    multiply(1)
    image_second = image - step * finish(1, image)

    sums_start(1, second * second, second * image_second)
    sums_pass(1)
    drain(0)
    drain(1)
    norm_second, curvature = sums_end(1)
    ratio = norm_second / norm_first
    step_second = norm_second / (curvature - ratio * norm_second / step)
    solution_ref[...] = step * first + step_second * (second + ratio * first)
    residual_ref[...] = second - step_second * (image_second + ratio * image)
    sums_drain(0)
    sums_drain(1)


def per_device(R, C, kernel_configs, epoch_kernel, lengths, noise, curves):
    rows, epochs = curves.shape
    L = R // INNER
    width = epochs // HALVES
    f32 = jnp.float32
    bf16 = jnp.bfloat16
    dma = pltpu.SemaphoreType.DMA
    return pl.pallas_call(
        functools.partial(kernel, R, C),
        out_shape=[jax.ShapeDtypeStruct((rows, epochs), f32)] * 2,
        in_specs=[pl.BlockSpec(memory_space=pl.ANY)] * 5,
        out_specs=[pl.BlockSpec(memory_space=pltpu.VMEM)] * 2,
        scratch_shapes=[
            pltpu.VMEM(kernel_configs.shape, f32),
            pltpu.VMEM((epochs, epochs), f32),
            pltpu.VMEM((1, rows), jnp.int32),
            pltpu.VMEM((1, rows), f32),
            pltpu.VMEM((rows, epochs), f32),
            pltpu.VMEM((C * rows, R * rows), bf16),
            pltpu.VMEM((C * rows, R * rows), bf16),
            pltpu.VMEM((epochs, epochs), bf16),
            pltpu.VMEM((epochs, epochs), bf16),
            pltpu.VMEM((2, HALVES, R, rows, width), f32),
            pltpu.VMEM((2, HALVES, C, rows, width), f32),
            pltpu.VMEM((2, HALVES, C - 1, rows, width), f32),
            pltpu.VMEM((2, C, 2, 8, 128), f32),
            pltpu.VMEM((2, R, 2, 8, 128), f32),
            dma((5,)),
            dma((2, HALVES, L)),
            dma((2, HALVES, L)),
            dma((2, HALVES, L)),
            dma((2, HALVES, L)),
            dma((2, HALVES, C)),
            dma((2, HALVES, C)),
            dma((2, C)),
            dma((2, C)),
            dma((2, R)),
            dma((2, R)),
        ],
        compiler_params=pltpu.CompilerParams(collective_id=0, has_side_effects=True),
        name="cg",
    )(kernel_configs, epoch_kernel, lengths.reshape(1, -1), noise.reshape(1, -1), curves)


def solution(mesh):
    in_specs = (
        P(None, "row", "col"),
        P(),
        P(("col", "row")),
        P(("col", "row")),
        P(("col", "row"), None),
    )
    out_specs = (P(("col", "row"), None), P(("col", "row"), None))
    body = functools.partial(per_device, mesh.shape["row"], mesh.shape["col"])
    return jax.shard_map(body, mesh=mesh, in_specs=in_specs, out_specs=out_specs, check_vma=False)
```

```python
import functools
import math

import jax
import jax.numpy as jnp
from jax import lax
from jax.experimental import pallas as pl
from jax.experimental.pallas import tpu as pltpu
from jax.sharding import PartitionSpec as P

MESH = pl.DeviceIdType.MESH
HALVES = 2
GROUP = 2


def flip(index, bits):
    place = 1
    result = index
    while place <= bits:
        if (bits // place) % 2:
            result = result + place * (1 - 2 * ((index // place) % 2))
        place *= 2
    return result


def split(value):
    high = value.astype(jnp.bfloat16)
    low = (value - high.astype(jnp.float32)).astype(jnp.bfloat16)
    return high, low


def dot3(left, right):
    mul = functools.partial(jnp.dot, preferred_element_type=jnp.float32)
    return mul(left[0], right[0]) + (mul(left[0], right[1]) + mul(left[1], right[0]))


def fold(value):
    rows, epochs = value.shape
    tiles = [
        value[i : i + 8, j : j + 128] for i in range(0, rows, 8) for j in range(0, epochs, 128)
    ]
    while len(tiles) > 1:
        tiles = [sum(tiles[i : i + 2][1:], tiles[i]) for i in range(0, len(tiles), 2)]
    return tiles[0]


def column(row):
    n = row.shape[1]
    one = lax.broadcasted_iota(jnp.int32, (n, n), 0)
    two = lax.broadcasted_iota(jnp.int32, (n, n), 1)
    return jnp.sum(jnp.where(one == two, row, jnp.zeros_like(row)), axis=1, keepdims=True)


def kernel(
    R, C,
    tile_hbm, epoch_hbm, lengths_hbm, noise_hbm, curves_hbm,
    solution_ref, residual_ref,
    tile, epoch, lengths, noise, curves,
    tile_high, tile_low, epoch_high, epoch_low,
    gathered, crossed, partial, arrived, sums,
    load_sem, row_send, row_recv,
    cross_send, cross_recv, part_send, part_recv, sums_send, sums_recv,
):
    N = R * C
    me_row = lax.axis_index("row")
    me_col = lax.axis_index("col")
    rows, epochs = curves.shape
    width = epochs // HALVES

    loads = []
    for i, (src, dst) in enumerate(
        ((curves_hbm, curves), (lengths_hbm, lengths), (noise_hbm, noise),
         (tile_hbm, tile), (epoch_hbm, epoch))
    ):
        load = pltpu.make_async_copy(src, dst, load_sem.at[i])
        load.start()
        loads.append(load)

    def row_target(d):
        return (flip(me_row, d), me_col)

    def col_target(j):
        return (me_row, flip(me_col, j))

    barrier = pltpu.get_barrier_semaphore()

    def greet(target):
        pl.semaphore_signal(barrier, inc=1, device_id=target, device_id_type=MESH)

    direct = [*range(GROUP, R, GROUP), *range(1, GROUP)]
    for d in direct:
        greet(row_target(d))
    for j in range(1, C):
        greet(col_target(j))

    for load in loads[:3]:
        load.wait()
    length_col = column(lengths[...].astype(jnp.float32))
    noise_col = column(noise[...])
    position = lax.broadcasted_iota(jnp.int32, (rows, epochs), 1).astype(jnp.float32)
    mask = position < length_col
    first = jnp.where(mask, curves[...], 0.0)

    def remote(src, dst, send, recv, target):
        return pltpu.make_async_remote_copy(
            src_ref=src, dst_ref=dst, send_sem=send, recv_sem=recv,
            device_id=target, device_id_type=MESH,
        )

    def row_copy(op, h, d):
        near = d % GROUP
        far = d - near
        held, step = (far, near) if far and near else (0, d)
        block = gathered.at[op, h, flip(me_row, held)]
        return remote(block, block, row_send.at[op, h, d], row_recv.at[op, h, d], row_target(step))

    def row_arrival(op, h, d):
        block = gathered.at[op, h, flip(me_row, d)]
        return remote(block, block, row_send.at[op, h, d], row_recv.at[op, h, d], row_target(1))

    def cross_copy(op, j, at):
        block = crossed.at[op, at]
        return remote(block, block, cross_send.at[op, j], cross_recv.at[op, j], col_target(j))

    def part_copy(op, h, j):
        return remote(
            partial.at[op, h, flip(me_col, j)], arrived.at[op, h, j - 1],
            part_send.at[op, h, j], part_recv.at[op, h, j], col_target(j),
        )

    def spread(op, field):
        for h in range(HALVES):
            gathered[op, h, me_row] = field[:, h * width : (h + 1) * width]
            for d in direct:
                row_copy(op, h, d).start()
        crossed[op, me_col] = field
        for j in range(1, C):
            cross_copy(op, j, me_col).start()

    def relay(op):
        for h in range(HALVES):
            for far in range(GROUP, R, GROUP):
                row_arrival(op, h, far).wait_recv()
                for near in range(1, GROUP):
                    row_copy(op, h, far + near).start()

    def multiply(op):
        for h in range(HALVES):
            for d in range(1, R):
                if d < GROUP or d % GROUP:
                    row_arrival(op, h, d).wait_recv()
            block = split(gathered[op, h].reshape(R * rows, width))
            product = dot3((tile_high[...], tile_low[...]), block)
            partial[op, h] = product.reshape(C, rows, width)
            for j in range(1, C):
                part_copy(op, h, j).start()

    def finish(op, field):
        smoothed = None
        for h in range(HALVES):
            value = partial[op, h, me_col]
            for j in range(1, C):
                part_copy(op, h, j).wait_recv()
                value = value + arrived[op, h, j - 1]
            cut = slice(h * width, (h + 1) * width)
            term = dot3(split(value), (epoch_high[cut, :], epoch_low[cut, :]))
            smoothed = term if smoothed is None else smoothed + term
        return jnp.where(mask, smoothed, 0.0) + noise_col * field

    def drain(op):
        for h in range(HALVES):
            for d in range(1, R):
                row_copy(op, h, d).wait_send()
            for j in range(1, C):
                part_copy(op, h, j).wait_send()
        for j in range(1, C):
            cross_copy(op, j, me_col).wait_send()

    def sums_start(t, one, two):
        sums[t, 0, :, :128] = jnp.sum(one, axis=0, keepdims=True)
        sums[t, 0, :, 128:] = jnp.sum(two, axis=0, keepdims=True)
        for d in range(1, N):
            remote(
                sums.at[t, 0], sums.at[t, d], sums_send.at[t], sums_recv.at[t],
                (flip(me_row, d // C), flip(me_col, d % C)),
            ).start()

    def sums_all(t):
        block = sums.at[t, pl.ds(1, N - 1)]
        return remote(block, block, sums_send.at[t], sums_recv.at[t], row_target(1))

    def sums_end(t):
        sums_all(t).wait_recv()
        value = sums[t, 0]
        for d in range(1, N):
            value = value + sums[t, d]
        return (
            jnp.sum(value[:, :128], axis=1, keepdims=True),
            jnp.sum(value[:, 128:], axis=1, keepdims=True),
        )

    pl.semaphore_wait(barrier, len(direct) + C - 1)
    spread(0, first)
    for load in loads[3:]:
        load.wait()
    high, low = split(tile[...].reshape(C * rows, R * rows))
    tile_high[...] = high
    tile_low[...] = low
    high, low = split(epoch[...])
    epoch_high[...] = high
    epoch_low[...] = low
    relay(0)
    multiply(0)
    image = finish(0, first)

    spread(1, image)
    sums_start(0, fold(first * first), fold(first * image))
    relay(1)
    norm_first, curvature = sums_end(0)
    step = norm_first / curvature
    second = first - step * image
    norm_tile = fold(second * second)
    noise_tile = fold(noise_col * second * second)
    for op in range(2):
        for j in range(1, C):
            cross_copy(op, j, flip(me_col, j)).wait_recv()
    weight = (crossed[0] - step * crossed[1]).reshape(C * rows, epochs)
    weight = dot3(split(weight), (epoch_high[...], epoch_low[...]))
    multiply(1)
    for h in range(HALVES):
        difference = (partial[0, h] - step * partial[1, h]).reshape(C * rows, width)
        noise_tile = noise_tile + fold(weight[:, h * width : (h + 1) * width] * difference)
    sums_start(1, norm_tile, noise_tile)
    image_second = image - step * finish(1, image)
    drain(0)
    drain(1)
    norm_second, curvature = sums_end(1)
    ratio = norm_second / norm_first
    step_second = norm_second / (curvature - ratio * norm_second / step)
    solution_ref[...] = step * first + step_second * (second + ratio * first)
    residual_ref[...] = second - step_second * (image_second + ratio * image)
    for t in range(2):
        sums_all(t).wait_send()


def per_device(R, C, kernel_configs, epoch_kernel, lengths, noise, curves):
    rows, epochs = curves.shape
    width = epochs // HALVES
    f32 = jnp.float32
    bf16 = jnp.bfloat16
    dma = pltpu.SemaphoreType.DMA
    buffers = [
        (kernel_configs.shape, f32),
        ((epochs, epochs), f32),
        ((1, rows), jnp.int32),
        ((1, rows), f32),
        ((rows, epochs), f32),
        ((C * rows, R * rows), bf16),
        ((C * rows, R * rows), bf16),
        ((epochs, epochs), bf16),
        ((epochs, epochs), bf16),
        ((2, HALVES, R, rows, width), f32),
        ((2, C, rows, epochs), f32),
        ((2, HALVES, C, rows, width), f32),
        ((2, HALVES, C - 1, rows, width), f32),
        ((2, R * C, 1, 256), f32),
    ]
    held = sum(math.prod(shape) * jnp.dtype(kind).itemsize for shape, kind in buffers)
    return pl.pallas_call(
        functools.partial(kernel, R, C),
        out_shape=[jax.ShapeDtypeStruct((rows, epochs), f32)] * 2,
        in_specs=[pl.BlockSpec(memory_space=pltpu.HBM)] * 5,
        out_specs=[pl.BlockSpec(memory_space=pltpu.VMEM)] * 2,
        scratch_shapes=[pltpu.VMEM(shape, kind) for shape, kind in buffers]
        + [
            dma((5,)),
            dma((2, HALVES, R)),
            dma((2, HALVES, R)),
            dma((2, C)),
            dma((2, C)),
            dma((2, HALVES, C)),
            dma((2, HALVES, C)),
            dma((2,)),
            dma((2,)),
        ],
        compiler_params=pltpu.CompilerParams(
            collective_id=0, has_side_effects=True,

        ),
        name="cg",
    )(kernel_configs, epoch_kernel, lengths.reshape(1, -1), noise.reshape(1, -1), curves)


def solution(mesh):
    in_specs = (
        P(None, "row", "col"),
        P(),
        P(("col", "row")),
        P(("col", "row")),
        P(("col", "row"), None),
    )
    out_specs = (P(("col", "row"), None), P(("col", "row"), None))
    body = functools.partial(per_device, mesh.shape["row"], mesh.shape["col"])
    return jax.shard_map(body, mesh=mesh, in_specs=in_specs, out_specs=out_specs, check_vma=False)
```

```python
import functools
import math

import jax
import jax.numpy as jnp
from jax import lax
from jax.experimental import pallas as pl
from jax.experimental.pallas import tpu as pltpu
from jax.sharding import PartitionSpec as P

MESH = pl.DeviceIdType.MESH
HALVES = 2
GROUP = 4


def flip(index, bits):
    place = 1
    result = index
    while place <= bits:
        if (bits // place) % 2:
            result = result + place * (1 - 2 * ((index // place) % 2))
        place *= 2
    return result


def split(value):
    high = value.astype(jnp.bfloat16)
    low = (value - high.astype(jnp.float32)).astype(jnp.bfloat16)
    return high, low


def dot3(left, right):
    mul = functools.partial(jnp.dot, preferred_element_type=jnp.float32)
    return mul(left[0], right[0]) + (mul(left[0], right[1]) + mul(left[1], right[0]))


def fold(value):
    rows, epochs = value.shape
    tiles = [
        value[i : i + 8, j : j + 128] for i in range(0, rows, 8) for j in range(0, epochs, 128)
    ]
    while len(tiles) > 1:
        tiles = [sum(tiles[i : i + 2][1:], tiles[i]) for i in range(0, len(tiles), 2)]
    return tiles[0]


def column(row):
    n = row.shape[1]
    one = lax.broadcasted_iota(jnp.int32, (n, n), 0)
    two = lax.broadcasted_iota(jnp.int32, (n, n), 1)
    return jnp.sum(jnp.where(one == two, row, jnp.zeros_like(row)), axis=1, keepdims=True)


def kernel(
    R, C,
    tile_hbm, epoch_hbm, lengths_hbm, noise_hbm, curves_hbm,
    solution_ref, residual_ref,
    tile, epoch, lengths, noise, curves,
    tile_high, tile_low, epoch_high, epoch_low,
    gathered, crossed, partial, arrived, sums,
    load_sem, row_send, row_recv,
    cross_send, cross_recv, part_send, part_recv, sums_send, sums_recv,
):
    N = R * C
    me_row = lax.axis_index("row")
    me_col = lax.axis_index("col")
    rows, epochs = curves.shape
    width = epochs // HALVES

    loads = []
    for i, (src, dst) in enumerate(
        ((curves_hbm, curves), (lengths_hbm, lengths), (noise_hbm, noise),
         (tile_hbm, tile), (epoch_hbm, epoch))
    ):
        load = pltpu.make_async_copy(src, dst, load_sem.at[i])
        load.start()
        loads.append(load)

    def row_target(d):
        return (flip(me_row, d), me_col)

    def col_target(j):
        return (me_row, flip(me_col, j))

    barrier = pltpu.get_barrier_semaphore()

    def greet(target):
        pl.semaphore_signal(barrier, inc=1, device_id=target, device_id_type=MESH)

    direct = [*range(GROUP, R, GROUP), 2, 1]
    for d in direct + [3]:
        greet(row_target(d))
    for j in range(1, C):
        greet(col_target(j))

    for load in loads[:3]:
        load.wait()
    length_col = column(lengths[...].astype(jnp.float32))
    noise_col = column(noise[...])
    position = lax.broadcasted_iota(jnp.int32, (rows, epochs), 1).astype(jnp.float32)
    mask = position < length_col
    first = jnp.where(mask, curves[...], 0.0)

    def remote(src, dst, send, recv, target):
        return pltpu.make_async_remote_copy(
            src_ref=src, dst_ref=dst, send_sem=send, recv_sem=recv,
            device_id=target, device_id_type=MESH,
        )

    def row_copy(op, h, d):
        near = d % GROUP
        far = d - near
        held, step = (far, near) if far and near else (2, 1) if d == 3 else (0, d)
        block = gathered.at[op, h, flip(me_row, held)]
        return remote(block, block, row_send.at[op, h, d], row_recv.at[op, h, d], row_target(step))

    def row_arrival(op, h, d):
        block = gathered.at[op, h, flip(me_row, d)]
        return remote(block, block, row_send.at[op, h, d], row_recv.at[op, h, d], row_target(1))

    def cross_copy(op, j, at):
        block = crossed.at[op, at]
        return remote(block, block, cross_send.at[op, j], cross_recv.at[op, j], col_target(j))

    def part_copy(op, h, j):
        return remote(
            partial.at[op, h, flip(me_col, j)], arrived.at[op, h, j - 1],
            part_send.at[op, h, j], part_recv.at[op, h, j], col_target(j),
        )

    def spread(op, field):
        for h in range(HALVES):
            gathered[op, h, me_row] = field[:, h * width : (h + 1) * width]
            for d in direct:
                row_copy(op, h, d).start()
        crossed[op, me_col] = field
        for j in range(1, C):
            cross_copy(op, j, me_col).start()

    def relay(op):
        for h in range(HALVES):
            for far in range(GROUP, R, GROUP):
                row_arrival(op, h, far).wait_recv()
                for near in (3, 1, 2):
                    row_copy(op, h, far + near).start()
            row_arrival(op, h, 2).wait_recv()
            row_copy(op, h, 3).start()

    def multiply(op):
        for h in range(HALVES):
            for d in range(1, R):
                if d != 2 and d % GROUP:
                    row_arrival(op, h, d).wait_recv()
            block = split(gathered[op, h].reshape(R * rows, width))
            product = dot3((tile_high[...], tile_low[...]), block)
            partial[op, h] = product.reshape(C, rows, width)
            for j in range(1, C):
                part_copy(op, h, j).start()

    def finish(op, field):
        smoothed = None
        for h in range(HALVES):
            value = partial[op, h, me_col]
            for j in range(1, C):
                part_copy(op, h, j).wait_recv()
                value = value + arrived[op, h, j - 1]
            cut = slice(h * width, (h + 1) * width)
            term = dot3(split(value), (epoch_high[cut, :], epoch_low[cut, :]))
            smoothed = term if smoothed is None else smoothed + term
        return jnp.where(mask, smoothed, 0.0) + noise_col * field

    def drain(op):
        for h in range(HALVES):
            for d in range(1, R):
                row_copy(op, h, d).wait_send()
            for j in range(1, C):
                part_copy(op, h, j).wait_send()
        for j in range(1, C):
            cross_copy(op, j, me_col).wait_send()

    def sums_start(t, one, two):
        sums[t, 0, :, :128] = jnp.sum(one, axis=0, keepdims=True)
        sums[t, 0, :, 128:] = jnp.sum(two, axis=0, keepdims=True)
        for d in range(1, N):
            remote(
                sums.at[t, 0], sums.at[t, d], sums_send.at[t], sums_recv.at[t],
                (flip(me_row, d // C), flip(me_col, d % C)),
            ).start()

    def sums_all(t):
        block = sums.at[t, pl.ds(1, N - 1)]
        return remote(block, block, sums_send.at[t], sums_recv.at[t], row_target(1))

    def sums_end(t):
        sums_all(t).wait_recv()
        value = sums[t, 0]
        for d in range(1, N):
            value = value + sums[t, d]
        return (
            jnp.sum(value[:, :128], axis=1, keepdims=True),
            jnp.sum(value[:, 128:], axis=1, keepdims=True),
        )

    pl.semaphore_wait(barrier, len(direct) + 1 + C - 1)
    spread(0, first)
    for load in loads[3:]:
        load.wait()
    high, low = split(tile[...].reshape(C * rows, R * rows))
    tile_high[...] = high
    tile_low[...] = low
    high, low = split(epoch[...])
    epoch_high[...] = high
    epoch_low[...] = low
    relay(0)
    multiply(0)
    image = finish(0, first)

    spread(1, image)
    sums_start(0, fold(first * first), fold(first * image))
    relay(1)
    norm_first, curvature = sums_end(0)
    step = norm_first / curvature
    second = first - step * image
    norm_tile = fold(second * second)
    noise_tile = fold(noise_col * second * second)
    for op in range(2):
        for j in range(1, C):
            cross_copy(op, j, flip(me_col, j)).wait_recv()
    weight = (crossed[0] - step * crossed[1]).reshape(C * rows, epochs)
    weight = dot3(split(weight), (epoch_high[...], epoch_low[...]))
    multiply(1)
    for h in range(HALVES):
        difference = (partial[0, h] - step * partial[1, h]).reshape(C * rows, width)
        noise_tile = noise_tile + fold(weight[:, h * width : (h + 1) * width] * difference)
    sums_start(1, norm_tile, noise_tile)
    image_second = image - step * finish(1, image)
    drain(0)
    drain(1)
    norm_second, curvature = sums_end(1)
    ratio = norm_second / norm_first
    step_second = norm_second / (curvature - ratio * norm_second / step)
    solution_ref[...] = step * first + step_second * (second + ratio * first)
    residual_ref[...] = second - step_second * (image_second + ratio * image)
    for t in range(2):
        sums_all(t).wait_send()


def per_device(R, C, kernel_configs, epoch_kernel, lengths, noise, curves):
    rows, epochs = curves.shape
    width = epochs // HALVES
    f32 = jnp.float32
    bf16 = jnp.bfloat16
    dma = pltpu.SemaphoreType.DMA
    buffers = [
        (kernel_configs.shape, f32),
        ((epochs, epochs), f32),
        ((1, rows), jnp.int32),
        ((1, rows), f32),
        ((rows, epochs), f32),
        ((C * rows, R * rows), bf16),
        ((C * rows, R * rows), bf16),
        ((epochs, epochs), bf16),
        ((epochs, epochs), bf16),
        ((2, HALVES, R, rows, width), f32),
        ((2, C, rows, epochs), f32),
        ((2, HALVES, C, rows, width), f32),
        ((2, HALVES, C - 1, rows, width), f32),
        ((2, R * C, 1, 256), f32),
    ]
    held = sum(math.prod(shape) * jnp.dtype(kind).itemsize for shape, kind in buffers)
    return pl.pallas_call(
        functools.partial(kernel, R, C),
        out_shape=[jax.ShapeDtypeStruct((rows, epochs), f32)] * 2,
        in_specs=[pl.BlockSpec(memory_space=pltpu.HBM)] * 5,
        out_specs=[pl.BlockSpec(memory_space=pltpu.VMEM)] * 2,
        scratch_shapes=[pltpu.VMEM(shape, kind) for shape, kind in buffers]
        + [
            dma((5,)),
            dma((2, HALVES, R)),
            dma((2, HALVES, R)),
            dma((2, C)),
            dma((2, C)),
            dma((2, HALVES, C)),
            dma((2, HALVES, C)),
            dma((2,)),
            dma((2,)),
        ],
        compiler_params=pltpu.CompilerParams(
            collective_id=0, has_side_effects=True,
            vmem_limit_bytes=min(2 * held + (8 << 20), 60 * 1024 * 1024),
        ),
        name="cg",
    )(*[
        pltpu.with_memory_space_constraint(value, pltpu.HBM)
        for value in (kernel_configs, epoch_kernel, lengths.reshape(1, -1), noise.reshape(1, -1), curves)
    ])


def solution(mesh):
    in_specs = (
        P(None, "row", "col"),
        P(),
        P(("col", "row")),
        P(("col", "row")),
        P(("col", "row"), None),
    )
    out_specs = (P(("col", "row"), None), P(("col", "row"), None))
    body = functools.partial(per_device, mesh.shape["row"], mesh.shape["col"])
    return jax.shard_map(body, mesh=mesh, in_specs=in_specs, out_specs=out_specs, check_vma=False)
```
